32 devices in a mesh: groups: 2 (over x), tm: 16 (over z, y, core).
Axes of the slice: x: 2, y: 2, z: 4, core: 2. Of those that a mesh axis runs over, the one named last changes fastest.
Arguments:
- states: bfloat16 [4096, 2, 1024], P('tm', 'groups'), parts along dimension 1, may hold values from -6 to 6
- goals: bfloat16 [4096, 2, 1024], P('tm', 'groups'), parts along dimension 1, may hold values from -6 to 6
- pos_offset: int32 [16, 2, 8], P('tm', 'groups'), parts along dimension 1, may hold values from 0 to 15
- neg_blocks: int32 [16, 2, 16], P('tm', 'groups'), parts along dimension 1, may hold values from 0 to 15
Outputs:
- loss_mean: float32 [2], P('groups'), parts along dimension 0
- grad_states: float32 [4096, 2, 1024], P('tm', 'groups'), parts along dimension 1
- grad_goals: float32 [4096, 2, 1024], P('tm', 'groups'), parts along dimension 1
The draws below stay inside these ranges and needn't reach their ends.
There are 2 independent parts, one for each index of `groups`. The reference program is written for one: setup_inputs(seed, part) draws one part's arguments, and reference() takes and returns one part's arrays. A program takes and returns all parts, laid end to end along the dimension named above; each array names one. Nothing has to cross between parts.
All inputs are finite; a program needn't handle non-finite values.
Results may differ from the reference program's by a relative error of at most 0.012.
Values may be sent and summed in bfloat16 or wider, within the bound.
No kernel may reach another device: no remote copies, remote signals or barrier semaphores. Data moves between devices by JAX's collectives and lax.ppermute only.
A program may use at most 128 MiB of HBM per device.

```python
import math
import jax
import jax.numpy as jnp
from jax import lax

E = 1024
L = 256
P_SIZE = 8
K = 16
TRAJ = 1
STEPS = 4096
N_TM = 16


def touch_ends(drawn, own_key, least, high):
    longest = drawn.shape.index(max(drawn.shape))
    spots = []
    for shift in (0, 1):
        where = [jax.random.randint(jax.random.fold_in(own_key, axis), (), 0, length) for axis, length in enumerate(drawn.shape)]
        where[longest] = (where[longest] + shift) % drawn.shape[longest]
        spots.append(tuple(where))
    return drawn.at[spots[0]].set(least).at[spots[1]].set(high)


def block_scale(key, shape, pieces, least, largest):
    level, own = 1.0, jax.random.fold_in(key, 6)
    for position, blocks in pieces:
        draws = jnp.exp(jax.random.uniform(jax.random.fold_in(own, position), (blocks,), jnp.float32, least / len(pieces), largest / len(pieces)))
        level = level * jnp.repeat(draws, shape[position] // blocks).reshape([-1 if axis == position else 1 for axis in range(len(shape))])
    return level


def noise(own_key, shape, spread, reach, cuts=(), kind=jnp.bfloat16):
    result = jax.random.normal(own_key, shape, jnp.float32) * spread
    if len(cuts) > 0:
        result = block_scale(own_key, shape, cuts, -0.22, 0.18) * result
    return jnp.clip(result, min=-reach, max=reach).astype(kind)


def setup_inputs(seed: int = 0, part: int = 0) -> dict:
    keys = jax.random.split(jax.random.key(seed), 5)
    part_keys = jax.random.split(jax.random.fold_in(keys[4], part), 5)
    return {
        "states": noise(part_keys[0], (STEPS, TRAJ, E), 1.0, 6.0, ((0, 16),)),
        "goals": noise(part_keys[1], (STEPS, TRAJ, E), 1.0, 6.0, ((0, 16),)),
        "pos_offset": touch_ends(jax.random.randint(part_keys[2], (N_TM, TRAJ, P_SIZE), 0, N_TM), jax.random.fold_in(part_keys[2], 1), 0, N_TM - 1).astype(jnp.int32),
        "neg_blocks": touch_ends(jax.random.randint(part_keys[3], (N_TM, TRAJ, K), 0, N_TM), jax.random.fold_in(part_keys[3], 1), 0, N_TM - 1).astype(jnp.int32),
    }


def pair_weights(pos_offset, neg_blocks, row_first, col_first, row_count, col_count):
    block_count = row_count // L
    row_blocks = row_first // L + jnp.arange(block_count, dtype=jnp.int32)
    col_times = col_first + jnp.arange(col_count, dtype=jnp.int32)
    col_blocks = col_times // L
    targets = row_blocks[:, None, None] + pos_offset
    pos_count = lax.optimization_barrier(jnp.sum((targets[..., None] == col_blocks).astype(jnp.float32), axis=2))
    neg_count = lax.optimization_barrier(jnp.sum((neg_blocks[..., None] == col_blocks).astype(jnp.float32), axis=2))
    pos_count = jnp.repeat(jnp.swapaxes(pos_count, 0, 1), L, axis=1)
    neg_count = jnp.repeat(jnp.swapaxes(neg_count, 0, 1), L, axis=1)
    row_times = row_first + jnp.arange(row_count, dtype=jnp.int32)
    later_mask = (col_times[None, :] > row_times[:, None]).astype(jnp.float32)
    return (pos_count * later_mask, neg_count)

def score_terms(anchor_rows, goal_rows, pos_weight, neg_weight):
    inv_root = 1.0 / math.sqrt(E)
    scores = jnp.einsum('qte,kte->tqk', anchor_rows.astype(jnp.float32), goal_rows.astype(jnp.float32)) * inv_root
    loss_sum = jnp.sum(pos_weight * jax.nn.softplus(-scores) + neg_weight * jax.nn.softplus(scores))
    slopes = neg_weight * jax.nn.sigmoid(scores) - pos_weight * jax.nn.sigmoid(-scores)
    return (loss_sum, (slopes * inv_root).astype(jnp.bfloat16))

def reference(states, goals, pos_offset, neg_blocks):
    steps_all = L * N_TM
    goal_float = goals.astype(jnp.float32)

    def device_step(totals, device_index):
        row_first = device_index * L
        anchor_rows = lax.dynamic_slice_in_dim(states, row_first, L, 0)
        pos_rows = lax.dynamic_slice_in_dim(pos_offset, device_index, 1, 0)
        neg_rows = lax.dynamic_slice_in_dim(neg_blocks, device_index, 1, 0)
        pos_weight, neg_weight = pair_weights(pos_rows, neg_rows, row_first, jnp.int32(0), L, steps_all)
        loss_sum, coeffs = score_terms(anchor_rows, goals, pos_weight, neg_weight)
        coeff_float = coeffs.astype(jnp.float32)
        grad_rows = jnp.einsum('tqk,kte->qte', coeff_float, goal_float)
        block_term = jnp.einsum('tqk,qte->kte', coeff_float, anchor_rows.astype(jnp.float32)).astype(jnp.bfloat16)
        block_term = lax.optimization_barrier(block_term).astype(jnp.float32)
        return ((totals[0] + block_term, totals[1] + loss_sum), grad_rows)
    start_totals = (jnp.zeros((steps_all, TRAJ, E), jnp.float32), jnp.zeros((), jnp.float32))
    totals, grad_blocks = lax.scan(device_step, start_totals, jnp.arange(N_TM, dtype=jnp.int32))
    grad_states = grad_blocks.reshape(steps_all, TRAJ, E)
    loss_mean = (totals[1] / (TRAJ * steps_all)).reshape(1)
    return (loss_mean, grad_states, totals[0])
```

```python
import functools
import math

import jax
import jax.numpy as jnp
from jax import lax
from jax.experimental import pallas as pl
from jax.experimental.pallas import tpu as pltpu
from jax.sharding import PartitionSpec as P

AXIS = "tm"


def swap(value, bit, size):
    return lax.ppermute(value, AXIS, [(i, i ^ bit) for i in range(size)])


def subsets(bits):
    found = [0]
    for bit in bits:
        found = found + [offset ^ bit for offset in found]
    return found


def tile_kernel(row_xors, col_xors, own_ref, *refs):
    n_row, n_col = len(row_xors), len(col_xors)
    pos_refs, refs = refs[:n_row], refs[n_row:]
    neg_refs, refs = refs[:n_row], refs[n_row:]
    row_hbm, refs = refs[:n_row], refs[n_row:]
    col_hbm, refs = refs[:n_col], refs[n_col:]
    loss_ref, refs = refs[0], refs[1:]
    row_out, refs = refs[:n_row], refs[n_row:]
    col_out, refs = refs[:n_col], refs[n_col:]
    rows, cols, coeff, row_grad, col_grad, in_sem, out_sem = refs
    length, width = row_hbm[0].shape
    inv_root = 1.0 / math.sqrt(width)
    own = own_ref[0]

    loads = []
    for i in range(n_row):
        loads.append(pltpu.make_async_copy(row_hbm[i], rows.at[pl.ds(i * length, length)], in_sem.at[i]))
    for j in range(n_col):
        loads.append(pltpu.make_async_copy(col_hbm[j], cols.at[pl.ds(j * length, length)], in_sem.at[n_row + j]))
    for load in loads:
        load.start()

    weights = []
    for i in range(n_row):
        block = own ^ row_xors[i]
        line = []
        for j in range(n_col):
            target = own ^ col_xors[j]
            pos = jnp.int32(0)
            for p in range(pos_refs[i].shape[0]):
                pos = pos + jnp.where(pos_refs[i][p] + block == target, 1, 0)
            neg = jnp.int32(0)
            for k in range(neg_refs[i].shape[0]):
                neg = neg + jnp.where(neg_refs[i][k] == target, 1, 0)
            line.append((pos.astype(jnp.float32), neg.astype(jnp.float32)))
        weights.append(line)

    for load in loads:
        load.wait()

    later = lax.broadcasted_iota(jnp.int32, (length, length), 1) > lax.broadcasted_iota(
        jnp.int32, (length, length), 0
    )
    loss = jnp.zeros((8, length), jnp.float32)
    for i in range(n_row):
        row_slice = pl.ds(i * length, length)
        for j in range(n_col):
            col_slice = pl.ds(j * length, length)
            scores = (
                lax.dot_general(
                    rows[row_slice, :], cols[col_slice, :], (((1,), (1,)), ((), ())),
                    preferred_element_type=jnp.float32,
                )
                * inv_root
            )
            pos, neg = weights[i][j]
            decay = jnp.exp(-jnp.abs(scores))
            whole = 1.0 + decay
            large = 1.0 / whole
            small = decay * large
            up = scores >= 0.0
            rise = jnp.where(up, large, small)
            fall = jnp.where(up, small, large)
            above = jnp.maximum(scores, 0.0)
            below = above - scores
            if row_xors[i] == col_xors[j]:
                pos_tile = jnp.where(later, pos, 0.0)
                soft = jnp.log(whole)
                part = pos_tile * (below + soft) + neg * (above + soft)
                coeffs = (neg * rise - pos_tile * fall) * inv_root
                while part.shape[0] > 8:
                    half = part.shape[0] // 2
                    part = part[:half] + part[half:]
            else:
                coeffs = (neg * inv_root) * rise - (pos * inv_root) * fall
                part = neg * above + pos * below
                while part.shape[0] > 8:
                    half = part.shape[0] // 2
                    part = part[:half] + part[half:]
                    whole = whole[:half] * whole[half:]
                part = part + (pos + neg) * jnp.log(whole)
            loss = loss + part
            coeff[row_slice, col_slice] = coeffs.astype(jnp.bfloat16)
        row_grad[row_slice, :] = jnp.dot(
            coeff[row_slice, :], cols[...], preferred_element_type=jnp.float32
        ).astype(row_grad.dtype)
        pltpu.make_async_copy(row_grad.at[row_slice], row_out[i], out_sem.at[i]).start()
    for j in range(n_col):
        col_slice = pl.ds(j * length, length)
        col_grad[col_slice, :] = lax.dot_general(
            coeff[:, col_slice], rows[...], (((0,), (0,)), ((), ())), preferred_element_type=jnp.float32
        ).astype(col_grad.dtype)
        pltpu.make_async_copy(col_grad.at[col_slice], col_out[j], out_sem.at[n_row + j]).start()
    loss_ref[0] = jnp.sum(loss)
    for i in range(n_row):
        pltpu.make_async_copy(row_grad.at[pl.ds(i * length, length)], row_out[i], out_sem.at[i]).wait()
    for j in range(n_col):
        pltpu.make_async_copy(
            col_grad.at[pl.ds(j * length, length)], col_out[j], out_sem.at[n_row + j]
        ).wait()


def tiles(own, pos, neg, rows, cols, row_xors, col_xors):
    n_row, n_col = len(rows), len(cols)
    length, width = rows[0].shape
    smem = pl.BlockSpec(memory_space=pltpu.SMEM)
    anywhere = pl.BlockSpec(memory_space=pl.ANY)
    block = jax.ShapeDtypeStruct((length, width), jnp.float32)
    flops = 6 * n_row * n_col * length * length * width
    return pl.pallas_call(
        functools.partial(tile_kernel, row_xors, col_xors),
        in_specs=[smem] * (1 + 2 * n_row) + [anywhere] * (n_row + n_col),
        out_specs=[smem] + [anywhere] * (n_row + n_col),
        out_shape=[jax.ShapeDtypeStruct((1,), jnp.float32)] + [block] * (n_row + n_col),
        scratch_shapes=[
            pltpu.VMEM((n_row * length, width), jnp.bfloat16),
            pltpu.VMEM((n_col * length, width), jnp.bfloat16),
            pltpu.VMEM((n_row * length, n_col * length), jnp.bfloat16),
            pltpu.VMEM((n_row * length, width), jnp.float32),
            pltpu.VMEM((n_col * length, width), jnp.float32),
            pltpu.SemaphoreType.DMA((n_row + n_col,)),
            pltpu.SemaphoreType.DMA((n_row + n_col,)),
        ],
        cost_estimate=pl.CostEstimate(
            flops=flops, bytes_accessed=6 * (n_row + n_col) * length * width,
            transcendentals=3 * n_row * n_col * length * length,
        ),
        compiler_params=pltpu.CompilerParams(vmem_limit_bytes=48 << 20),
        name="tiles",
    )(own, *pos, *neg, *rows, *cols)


def per_device(states, goals, pos_offset, neg_blocks):
    size = lax.axis_size(AXIS)
    length, width = states.shape[0], states.shape[2]
    high = size // 2
    inner = []
    bit = size // 4
    while bit > 1:
        inner.append(bit)
        bit //= 2
    row_xors, col_xors = [0, 1, high, high ^ 1], subsets(inner)
    state, goal = states.reshape(length, width), goals.reshape(length, width)
    table = jnp.concatenate([pos_offset.reshape(-1), neg_blocks.reshape(-1)])
    n_pos = pos_offset.size

    pair = swap(state, high, size)
    cols = [goal]
    for bit in inner:
        cols = cols + [swap(c, bit, size) for c in cols]
    pair_table = swap(table, high, size)
    rows = [state, swap(state, 1, size), pair, swap(pair, 1, size)]
    tables = [table, swap(table, 1, size), pair_table, swap(pair_table, 1, size)]
    own = lax.axis_index(AXIS).astype(jnp.int32).reshape(1)
    outs = tiles(
        own, [t[:n_pos] for t in tables], [t[n_pos:] for t in tables], rows, cols, row_xors, col_xors
    )
    loss, row_parts, col_parts = outs[0], outs[1:5], outs[5:]

    here = row_parts[0] + swap(row_parts[1].astype(jnp.bfloat16), 1, size)
    there = row_parts[2] + swap(row_parts[3].astype(jnp.bfloat16), 1, size)
    grad_states = here + swap(there.astype(jnp.bfloat16), high, size)

    parts = dict(zip(col_xors, col_parts))
    for bit in reversed(inner):
        moved = {k: swap(v.astype(jnp.bfloat16), bit, size) for k, v in parts.items() if k & bit}
        parts = {k: v + moved[k ^ bit].astype(jnp.float32) for k, v in parts.items() if not k & bit}
    grad_goals = parts[0]

    bit = 1
    while bit < size:
        loss = loss + swap(loss, bit, size)
        bit *= 2
    loss_mean = loss / (size * length)
    return (
        loss_mean,
        grad_states.reshape(length, 1, width),
        grad_goals.reshape(length, 1, width),
    )


def solution(mesh):
    spec = P("tm", "groups", None)
    return jax.shard_map(
        per_device,
        mesh=mesh,
        in_specs=(spec,) * 4,
        out_specs=(P("groups"), spec, spec),
        check_vma=False,
    )
```

```python
import functools
import math

import jax
import jax.numpy as jnp
from jax import lax
from jax.experimental import pallas as pl
from jax.experimental.pallas import tpu as pltpu
from jax.sharding import PartitionSpec as P


AXIS = "tm"


def swap(value, offset, size, only=lambda i: True):
    return lax.ppermute(value, AXIS, [(i, i ^ offset) for i in range(size) if only(i)])


def subsets(bits):
    found = [0]
    for bit in bits:
        found = found + [offset ^ bit for offset in found]
    return found


def fold(part, op):
    pieces = [part[k : k + 8] for k in range(0, part.shape[0], 8)]
    while len(pieces) > 1:
        pieces = [op(*pieces[k : k + 2]) if k + 1 < len(pieces) else pieces[k] for k in range(0, len(pieces), 2)]
    return pieces[0]


def tile_kernel(plan, own_ref, *refs):
    n_new = len(plan["row_places"]) + len(plan["col_places"])
    tables, refs = refs[: plan["n_tables"]], refs[plan["n_tables"] :]
    arrived, refs = refs[:n_new], refs[n_new:]
    if plan["aliased"] or not plan["new"]:
        held, refs = refs[:3], refs[3:]
    if plan["new"]:
        loss_ref, held, refs = refs[0], refs[1:4], refs[4:]
    rows, cols, coeff = held
    row_out, refs = refs[: len(plan["row_outs"])], refs[len(plan["row_outs"]) :]
    col_out, (fresh, sem) = refs[: len(plan["col_outs"])], refs[len(plan["col_outs"]) :]
    width = rows.shape[1]
    inv_root = 1.0 / math.sqrt(width)
    size = tables[0].shape[0] // 2 if tables else 0

    targets = [rows.at[pl.ds(p, r.shape[0])] for p, r in zip(plan["row_places"], arrived)]
    targets += [cols.at[pl.ds(p, r.shape[0])] for p, r in zip(plan["col_places"], arrived[len(targets) :])]
    loads = [pltpu.make_async_copy(s, t, sem.at[k]) for k, (s, t) in enumerate(zip(arrived, targets))]
    for copy in loads:
        copy.start()
    for copy in loads:
        copy.wait()

    if plan["new"]:
        own = own_ref[0]
        loss = jnp.zeros((8, 128), jnp.float32)
        at, kept = 0, []
        for r0, r1, c0, c1 in plan["new"]:
            buffer = fresh.at[pl.ds(0, r1 - r0), pl.ds(at, c1 - c0)]
            at += c1 - c0
            kept.append((buffer, coeff.at[pl.ds(r0, r1 - r0), pl.ds(c0, c1 - c0)]))
            for cp, cl, j, c_off in plan["col_chunks"]:
                if cp < c0 or cp >= c1:
                    continue
                dots = (
                    lax.dot_general(
                        rows[r0:r1, :], cols[cp : cp + cl, :], (((1,), (1,)), ((), ())),
                        preferred_element_type=jnp.float32,
                    )
                    * inv_root
                )
                target = own ^ plan["col_xors"][j]
                for rp, rl, i, r_off in plan["row_chunks"]:
                    if rp < r0 or rp >= r1:
                        continue
                    scores = dots[rp - r0 : rp - r0 + rl]
                    pos, neg = tables[i][target], tables[i][size + target]
                    decay = jnp.exp(-jnp.abs(scores))
                    whole = 1.0 + decay
                    large = 1.0 / whole
                    up = scores >= 0.0
                    above = jnp.maximum(scores, 0.0)
                    if plan["row_xors"][i] == plan["col_xors"][j]:
                        later = lax.broadcasted_iota(jnp.int32, scores.shape, 1) + c_off > (
                            lax.broadcasted_iota(jnp.int32, scores.shape, 0) + r_off
                        )
                        pos = jnp.where(later, pos, 0.0)
                        soft = jnp.log(whole)
                        part = fold(pos * (above - scores + soft) + neg * (above + soft), jnp.add)
                    else:
                        over, total = fold(above, jnp.add), fold(scores, jnp.add)
                        part = neg * over + pos * (over - total)
                        part = part + (pos + neg) * jnp.log(fold(whole, jnp.multiply))
                    gain, drop = neg * inv_root, pos * inv_root
                    values = (jnp.where(up, gain, -drop) + jnp.where(up, -drop, gain) * decay) * large
                    for k in range(0, part.shape[1], 128):
                        loss = loss + part[:, k : k + 128]
                    buffer[rp - r0 : rp - r0 + rl, cp - c0 : cp - c0 + cl] = values.astype(jnp.bfloat16)
        loss_ref[...] = loss
        copies = [pltpu.make_async_copy(s, t, sem.at[n_new + k]) for k, (s, t) in enumerate(kept)]
        for copy in copies:
            copy.start()
        for copy in copies:
            copy.wait()

    def finish(outs, pieces, compute):
        if not outs:
            return
        low, high = min(p[0] for out in pieces for p in out), max(p[1] for out in pieces for p in out)
        for base in range(low, high, plan["step"]):
            top = min(high, base + plan["step"])
            value = compute(base, top)
            for out, parts in zip(outs, pieces):
                at = 0
                for p0, p1 in parts:
                    a, b = max(p0, base), min(p1, top)
                    if a < b:
                        out[at + a - p0 : at + b - p0, :] = value[a - base : b - base].astype(out.dtype)
                    at += p1 - p0

    finish(row_out, plan["row_outs"], lambda a, b: jnp.dot(
        coeff[a:b, :], cols[...], preferred_element_type=jnp.float32))
    finish(col_out, plan["col_outs"], lambda a, b: lax.dot_general(
        coeff[:, a:b], rows[...], (((0,), (0,)), ((), ())), preferred_element_type=jnp.float32))


def phase(own, tables, rows, cols, held, row_chunks, col_chunks, row_xors, col_xors, new=(), row_outs=(),
          col_outs=(), dtypes=None):
    n_row, n_col = (sum(c[1] for c in chunks) for chunks in (row_chunks, col_chunks))
    tables = tables if new else []
    width = next(iter(rows.values())).shape[1] if rows else held[0].shape[1]
    plan = dict(
        row_chunks=row_chunks, col_chunks=col_chunks, row_xors=row_xors, col_xors=col_xors, n_tables=len(tables),
        row_places=list(rows), col_places=list(cols), aliased=held is not None, new=new, row_outs=row_outs,
        col_outs=col_outs, step=512,
    )
    smem, anywhere, vmem = (pl.BlockSpec(memory_space=m) for m in (pltpu.SMEM, pl.ANY, pltpu.VMEM))
    args = [own, *tables, *rows.values(), *cols.values()]
    in_specs = [smem] * (1 + len(tables)) + [anywhere] * (len(rows) + len(cols))
    out_shape, aliases = [], {}
    if new:
        out_shape.append(pltpu.VMEM((8, 128), jnp.float32))
        if held is not None:
            aliases = {len(args) + k: 1 + k for k in range(3)}
        out_shape += [
            pltpu.VMEM(shape, jnp.bfloat16) for shape in ((n_row, width), (n_col, width), (n_row, n_col))
        ]
    if held is not None:
        args += [pltpu.with_memory_space_constraint(x, pltpu.VMEM) for x in held]
        in_specs += [vmem] * 3
    outs = (*row_outs, *col_outs)
    lengths = [sum(b - a for a, b in out) for out in outs]
    dtypes = dtypes or [jnp.bfloat16] * len(lengths)
    out_shape += [pltpu.VMEM((n, width), dtype) for n, dtype in zip(lengths, dtypes)]
    row_total, col_total = sum(lengths[: len(row_outs)]), sum(lengths[len(row_outs) :])
    area = sum((r1 - r0) * (c1 - c0) for r0, r1, c0, c1 in new)
    flops = 2 * width * (area + row_total * n_col + col_total * n_row)
    outs = list(
        pl.pallas_call(
            functools.partial(tile_kernel, plan),
            in_specs=in_specs,
            out_specs=[vmem] * len(out_shape),
            out_shape=out_shape,
            input_output_aliases=aliases,
            scratch_shapes=[
                pltpu.VMEM(
                    (max([16] + [r1 - r0 for r0, r1, _, _ in new]), max(128, sum(c1 - c0 for _, _, c0, c1 in new))),
                    jnp.bfloat16,
                ),
                pltpu.SemaphoreType.DMA((max(1, len(rows) + len(cols) + len(new)),)),
            ],
            cost_estimate=pl.CostEstimate(flops=flops, bytes_accessed=4 * width * width, transcendentals=2 * area),
            compiler_params=pltpu.CompilerParams(vmem_limit_bytes=20 << 20),
        )(*args)
    )
    loss = outs.pop(0) if new else None
    if new:
        held, outs = outs[:3], outs[3:]
    return loss, held, outs[: len(row_outs)], outs[len(row_outs) :]


def counts(pos_offset, neg_blocks, size):
    blocks = jnp.arange(size, dtype=jnp.int32)
    target = lax.axis_index(AXIS).astype(jnp.int32) + pos_offset.reshape(-1)
    pos = jnp.sum((target[:, None] == blocks).astype(jnp.float32), axis=0)
    neg = jnp.sum((neg_blocks.reshape(-1)[:, None] == blocks).astype(jnp.float32), axis=0)
    return jnp.concatenate([pos, neg])


def sum_kernel(groups, *refs):
    n_in = sum(len(group) for group in groups)
    ins, outs, totals, sem = list(refs[:n_in]), refs[n_in : n_in + len(groups)], refs[n_in + len(groups) : -1], refs[-1]
    n, stores = 64, []
    for starts, out, total in zip(groups, outs, totals):
        parts = [(start, ins.pop(0)) for start in starts]
        for r in range(0, out.shape[0], n):
            here = pl.ds(r, n)
            value = sum(
                part[r - start : r - start + n, :].astype(jnp.float32)
                for start, part in parts
                if start <= r < start + part.shape[0]
            )
            total[here] = value.reshape(n, *total.shape[1:])
            stores.append(pltpu.make_async_copy(total.at[here], out.at[here], sem.at[len(stores)]))
            stores[-1].start()
    for copy in stores:
        copy.wait()


def add_kernel(*refs):
    *parts, out = refs
    out[...] = sum(part[...].astype(jnp.float32) for part in parts).astype(out.dtype)


def add(*parts):
    vmem = pl.BlockSpec(memory_space=pltpu.VMEM)
    return pl.pallas_call(
        add_kernel,
        in_specs=[vmem] * len(parts),
        out_specs=vmem,
        out_shape=pltpu.VMEM(parts[0].shape, jnp.bfloat16),
        cost_estimate=pl.CostEstimate(
            flops=parts[0].size * len(parts), bytes_accessed=4 * parts[0].size, transcendentals=0
        ),
        compiler_params=pltpu.CompilerParams(vmem_limit_bytes=4 << 20),
    )(*[pltpu.with_memory_space_constraint(part, pltpu.VMEM) for part in parts])


def finish_sums(groups, length):
    width, lanes = groups[0][0][1].shape[1], 128
    anywhere, vmem = pl.BlockSpec(memory_space=pl.ANY), pl.BlockSpec(memory_space=pltpu.VMEM)
    flat = [part for group in groups for _, part in group]
    shape = (length, width // lanes, lanes)
    outs = pl.pallas_call(
        functools.partial(sum_kernel, [[start for start, _ in group] for group in groups]),
        in_specs=[vmem] * len(flat),
        out_specs=[anywhere] * len(groups),
        out_shape=[jax.ShapeDtypeStruct(shape, jnp.float32)] * len(groups),
        scratch_shapes=[pltpu.VMEM(shape, jnp.float32)] * len(groups)
        + [pltpu.SemaphoreType.DMA((len(groups) * (length // 64),))],
        cost_estimate=pl.CostEstimate(flops=6 * length * width, bytes_accessed=20 * length * width, transcendentals=0),
        compiler_params=pltpu.CompilerParams(vmem_limit_bytes=16 << 20),
    )(*[pltpu.with_memory_space_constraint(x, pltpu.VMEM) for x in flat])
    return [out.reshape(length, 1, width) for out in outs]


def step(states, goals, pos_offset, neg_blocks):
    size = lax.axis_size(AXIS)
    length, width = states.shape[0], states.shape[2]
    half = length // 2
    high = size // 2
    inner = []
    bit = size // 4
    while bit > 1:
        inner.append(bit)
        bit //= 2
    across = high ^ (high >> 1)
    row_xors, col_xors = [0, 1, across, across ^ 1], subsets(inner)
    n_row, n_col = len(row_xors) * length, len(col_xors) * length
    last = n_col - length
    state, goal = states.reshape(length, width), goals.reshape(length, width)
    own = lax.axis_index(AXIS).astype(jnp.int32).reshape(1)

    cols = {0: goal}
    for bit in inner:
        shift = len(cols) * length
        cols = {**cols, **{p + shift: swap(c, bit, size) for p, c in cols.items()}}
    sib = swap(state, 1, size)


    def outer(i):
        return (i & across) in (0, across)

    pair_in = swap(state, across, size, lambda i: not outer(i))
    pair = pair_in + swap(state, across, size, outer)
    far = swap(pair, 1, size)
    table = counts(pos_offset, neg_blocks, size)
    tables = [table] + [swap(table, x, size) for x in row_xors[1:]]

    near, third = 2 * length, 3 * length
    row_chunks = tuple((k * length, length, k, 0) for k in range(len(row_xors)))
    col_chunks = tuple((k * length, length, k, 0) for k in range(len(col_xors)))
    fixed = dict(row_chunks=row_chunks, col_chunks=col_chunks, row_xors=row_xors, col_xors=col_xors)
    early = {p: c for p, c in cols.items() if 0 < p < last}
    loss_a, held, _, _ = phase(
        own, tables[:2], {0: state, length: sib}, {0: goal}, None, new=[(0, near, 0, length)], **fixed
    )
    loss_b, held, _, _ = phase(own, tables[:2], {}, early, held, new=[(0, near, length, last)], **fixed)
    loss_e, held, _, _ = phase(own, tables[:2], {}, {last: cols[last]}, held, new=[(0, near, last, n_col)], **fixed)
    first = n_col // 2
    soon_cols = [[(first, first + half)], [(first + half, first + length)]]
    loss_c, held, _, soon = phase(
        own, tables, {near: pair, third: far}, {}, held, new=[(near, n_row, 0, last)], col_outs=soon_cols, **fixed
    )
    loss_d, held, (far_part, pair_part), _ = phase(
        own, tables, {}, {}, held, new=[(near, n_row, last, n_col)],
        row_outs=[[(third, n_row)], [(near, third)]], **fixed,
    )
    loss = loss_a + loss_b + loss_c + loss_d + loss_e

    back_far = swap(far_part, 1, size)
    loss = loss + swap(loss, across, size)
    back_pair = swap(add(pair_part, back_far), across, size)
    sent_cols = [[(p, p + half)] for p in range(first + length, n_col, half)]
    _, _, _, sent = phase(own, [], {}, {}, held, col_outs=sent_cols, **fixed)
    parts = {out[0][0]: value for out, value in zip([*soon_cols, *sent_cols], [*soon, *sent])}
    kept_cols = [[(0, length)]] + [[(p, p + half)] for p in range(length, n_col // 2, half)]
    _, _, (own_part, sib_part), kept = phase(
        own, [], {}, {}, held, row_outs=[[(0, length)], [(length, near)]], col_outs=kept_cols,
        dtypes=[jnp.float32, jnp.bfloat16] + [jnp.float32] * len(kept_cols), **fixed,
    )
    parts.update({out[0][0]: value for out, value in zip(kept_cols, kept)})
    back_sib = swap(sib_part, 1, size)
    for k, bit in reversed(list(enumerate(inner))):
        loss = loss + swap(loss, bit, size)
    loss = loss + swap(loss, 1, size)
    got = {}
    for k in reversed(range(len(inner))):
        lower = length << k
        for p in sorted(p - lower for p in parts if p >= lower)[::-1]:
            mine = parts.pop(p + lower)
            if p + lower in got:
                mine = add(mine, *got.pop(p + lower))
            got.setdefault(p, []).append(swap(mine, inner[k], size))
    goal_parts = [(0, parts[0])] + [(p, part) for p, received in got.items() for part in received]
    grad_states, grad_goals = finish_sums([[(0, own_part), (0, back_sib), (0, back_pair)], goal_parts], length)
    loss_mean = jnp.sum(loss).reshape(1) / (size * length)
    return (loss_mean, grad_states, grad_goals)


def solution(mesh):
    spec = P("tm", "groups", None)
    return jax.shard_map(
        step,
        mesh=mesh,
        in_specs=(spec,) * 4,
        out_specs=(P("groups"), spec, spec),
        check_vma=False,
    )
```

```python
import functools
import math

import jax
import jax.numpy as jnp
from jax import lax
from jax.experimental import pallas as pl
from jax.experimental.pallas import tpu as pltpu
from jax.sharding import PartitionSpec as P


AXIS = "tm"


def swap(value, offset, size, only=lambda i: True):
    return lax.ppermute(value, AXIS, [(i, i ^ offset) for i in range(size) if only(i)])


def subsets(bits):
    found = [0]
    for bit in bits:
        found = found + [offset ^ bit for offset in found]
    return found


def fold(part, op):
    pieces = [part[k : k + 8] for k in range(0, part.shape[0], 8)]
    while len(pieces) > 1:
        pieces = [op(*pieces[k : k + 2]) if k + 1 < len(pieces) else pieces[k] for k in range(0, len(pieces), 2)]
    return pieces[0]


def tile_kernel(plan, own_ref, *refs):
    n_new = len(plan["row_places"]) + len(plan["col_places"])
    tables, refs = refs[: plan["n_tables"]], refs[plan["n_tables"] :]
    arrived, refs = refs[:n_new], refs[n_new:]
    if plan["aliased"] or not plan["new"]:
        held, refs = refs[:3], refs[3:]
    if plan["new"]:
        loss_ref, held, refs = refs[0], refs[1:4], refs[4:]
    rows, cols, coeff = held
    row_out, refs = refs[: len(plan["row_outs"])], refs[len(plan["row_outs"]) :]
    col_out, (fresh, sem) = refs[: len(plan["col_outs"])], refs[len(plan["col_outs"]) :]
    width = rows.shape[1]
    inv_root = 1.0 / math.sqrt(width)
    size = tables[0].shape[0] // 2 if tables else 0

    targets = [rows.at[pl.ds(p, r.shape[0])] for p, r in zip(plan["row_places"], arrived)]
    targets += [cols.at[pl.ds(p, r.shape[0])] for p, r in zip(plan["col_places"], arrived[len(targets) :])]
    loads = [pltpu.make_async_copy(s, t, sem.at[k]) for k, (s, t) in enumerate(zip(arrived, targets))]
    for copy in loads:
        copy.start()
    for copy in loads:
        copy.wait()

    if plan["new"]:
        own = own_ref[0]
        loss = jnp.zeros((8, 128), jnp.float32)
        at, kept = 0, []
        for r0, r1, c0, c1 in plan["new"]:
            buffer = fresh.at[pl.ds(0, r1 - r0), pl.ds(at, c1 - c0)]
            at += c1 - c0
            kept.append((buffer, coeff.at[pl.ds(r0, r1 - r0), pl.ds(c0, c1 - c0)]))
            for cp, cl, j, c_off in plan["col_chunks"]:
                if cp < c0 or cp >= c1:
                    continue
                dots = (
                    lax.dot_general(
                        rows[r0:r1, :], cols[cp : cp + cl, :], (((1,), (1,)), ((), ())),
                        preferred_element_type=jnp.float32,
                    )
                    * inv_root
                )
                target = own ^ plan["col_xors"][j]
                for rp, rl, i, r_off in plan["row_chunks"]:
                    if rp < r0 or rp >= r1:
                        continue
                    scores = dots[rp - r0 : rp - r0 + rl]
                    pos, neg = tables[i][target], tables[i][size + target]
                    decay = jnp.exp(-jnp.abs(scores))
                    whole = 1.0 + decay
                    large = 1.0 / whole
                    up = scores >= 0.0
                    above = jnp.maximum(scores, 0.0)
                    if plan["row_xors"][i] == plan["col_xors"][j]:
                        later = lax.broadcasted_iota(jnp.int32, scores.shape, 1) + c_off > (
                            lax.broadcasted_iota(jnp.int32, scores.shape, 0) + r_off
                        )
                        pos = jnp.where(later, pos, 0.0)
                        soft = jnp.log(whole)
                        part = fold(pos * (above - scores + soft) + neg * (above + soft), jnp.add)
                    else:
                        over, total = fold(above, jnp.add), fold(scores, jnp.add)
                        part = neg * over + pos * (over - total)
                        part = part + (pos + neg) * jnp.log(fold(whole, jnp.multiply))
                    gain, drop = neg * inv_root, pos * inv_root
                    values = (jnp.where(up, gain, -drop) + jnp.where(up, -drop, gain) * decay) * large
                    for k in range(0, part.shape[1], 128):
                        loss = loss + part[:, k : k + 128]
                    buffer[rp - r0 : rp - r0 + rl, cp - c0 : cp - c0 + cl] = values.astype(jnp.bfloat16)
        loss_ref[...] = loss
        copies = [pltpu.make_async_copy(s, t, sem.at[n_new + k]) for k, (s, t) in enumerate(kept)]
        for copy in copies:
            copy.start()
        for copy in copies:
            copy.wait()

    def finish(outs, pieces, compute):
        if not outs:
            return
        low, high = min(p[0] for out in pieces for p in out), max(p[1] for out in pieces for p in out)
        for base in range(low, high, plan["step"]):
            top = min(high, base + plan["step"])
            value = compute(base, top)
            for out, parts in zip(outs, pieces):
                at = 0
                for p0, p1 in parts:
                    a, b = max(p0, base), min(p1, top)
                    if a < b:
                        out[at + a - p0 : at + b - p0, :] = value[a - base : b - base].astype(out.dtype)
                    at += p1 - p0

    finish(row_out, plan["row_outs"], lambda a, b: jnp.dot(
        coeff[a:b, :], cols[...], preferred_element_type=jnp.float32))
    finish(col_out, plan["col_outs"], lambda a, b: lax.dot_general(
        coeff[:, a:b], rows[...], (((0,), (0,)), ((), ())), preferred_element_type=jnp.float32))


def phase(own, tables, rows, cols, held, row_chunks, col_chunks, row_xors, col_xors, new=(), row_outs=(),
          col_outs=(), dtypes=None):
    n_row, n_col = (sum(c[1] for c in chunks) for chunks in (row_chunks, col_chunks))
    tables = tables if new else []
    width = next(iter(rows.values())).shape[1] if rows else held[0].shape[1]
    plan = dict(
        row_chunks=row_chunks, col_chunks=col_chunks, row_xors=row_xors, col_xors=col_xors, n_tables=len(tables),
        row_places=list(rows), col_places=list(cols), aliased=held is not None, new=new, row_outs=row_outs,
        col_outs=col_outs, step=512,
    )
    smem, anywhere, vmem = (pl.BlockSpec(memory_space=m) for m in (pltpu.SMEM, pl.ANY, pltpu.VMEM))
    args = [own, *tables, *rows.values(), *cols.values()]
    in_specs = [smem] * (1 + len(tables)) + [anywhere] * (len(rows) + len(cols))
    out_shape, aliases = [], {}
    if new:
        out_shape.append(pltpu.VMEM((8, 128), jnp.float32))
        if held is not None:
            aliases = {len(args) + k: 1 + k for k in range(3)}
        out_shape += [
            pltpu.VMEM(shape, jnp.bfloat16) for shape in ((n_row, width), (n_col, width), (n_row, n_col))
        ]
    if held is not None:
        args += [pltpu.with_memory_space_constraint(x, pltpu.VMEM) for x in held]
        in_specs += [vmem] * 3
    outs = (*row_outs, *col_outs)
    lengths = [sum(b - a for a, b in out) for out in outs]
    dtypes = dtypes or [jnp.bfloat16] * len(lengths)
    out_shape += [pltpu.VMEM((n, width), dtype) for n, dtype in zip(lengths, dtypes)]
    row_total, col_total = sum(lengths[: len(row_outs)]), sum(lengths[len(row_outs) :])
    area = sum((r1 - r0) * (c1 - c0) for r0, r1, c0, c1 in new)
    flops = 2 * width * (area + row_total * n_col + col_total * n_row)
    outs = list(
        pl.pallas_call(
            functools.partial(tile_kernel, plan),
            in_specs=in_specs,
            out_specs=[vmem] * len(out_shape),
            out_shape=out_shape,
            input_output_aliases=aliases,
            scratch_shapes=[
                pltpu.VMEM(
                    (max([16] + [r1 - r0 for r0, r1, _, _ in new]), max(128, sum(c1 - c0 for _, _, c0, c1 in new))),
                    jnp.bfloat16,
                ),
                pltpu.SemaphoreType.DMA((max(1, len(rows) + len(cols) + len(new)),)),
            ],
            cost_estimate=pl.CostEstimate(flops=flops, bytes_accessed=4 * width * width, transcendentals=2 * area),
            compiler_params=pltpu.CompilerParams(vmem_limit_bytes=20 << 20),
        )(*args)
    )
    loss = outs.pop(0) if new else None
    if new:
        held, outs = outs[:3], outs[3:]
    return loss, held, outs[: len(row_outs)], outs[len(row_outs) :]


def counts(pos_offset, neg_blocks, size):
    blocks = jnp.arange(size, dtype=jnp.int32)
    target = lax.axis_index(AXIS).astype(jnp.int32) + pos_offset.reshape(-1)
    pos = jnp.sum((target[:, None] == blocks).astype(jnp.float32), axis=0)
    neg = jnp.sum((neg_blocks.reshape(-1)[:, None] == blocks).astype(jnp.float32), axis=0)
    return jnp.concatenate([pos, neg])


def add_kernel(starts, *refs):
    *parts, out = refs
    out[...] = sum(
        part[start : start + out.shape[0], :].astype(jnp.float32) for start, part in zip(starts, parts)
    ).astype(out.dtype)


def add(rows, *parts):
    vmem = pl.BlockSpec(memory_space=pltpu.VMEM)
    width = parts[0][0].shape[1]
    return pl.pallas_call(
        functools.partial(add_kernel, [start for _, start in parts]),
        in_specs=[vmem] * len(parts),
        out_specs=vmem,
        out_shape=pltpu.VMEM((rows, width), jnp.bfloat16),
        cost_estimate=pl.CostEstimate(
            flops=rows * width * len(parts), bytes_accessed=4 * rows * width, transcendentals=0
        ),
        compiler_params=pltpu.CompilerParams(vmem_limit_bytes=4 << 20),
    )(*[pltpu.with_memory_space_constraint(part, pltpu.VMEM) for part, _ in parts])


def finish_kernel(groups, n_loss, count, *refs):
    n_in = sum(len(group) for group in groups)
    losses, ins, refs = refs[:n_loss], list(refs[n_loss : n_loss + n_in]), refs[n_loss + n_in :]
    loss_ref, outs, totals, sem = refs[0], refs[1 : 1 + len(groups)], refs[1 + len(groups) : -1], refs[-1]
    n, stores = 64, []
    for starts, out, total in zip(groups, outs, totals):
        parts = [(start, ins.pop(0)) for start in starts]
        lanes = total.shape[2]
        for r in range(0, out.shape[0], n):
            here = pl.ds(r, n)
            value = sum(
                part[r - start : r - start + n, :].astype(jnp.float32)
                for start, part in parts
                if start <= r < start + part.shape[0]
            )
            for k in range(total.shape[1]):
                total[here, k, :] = value[:, k * lanes : (k + 1) * lanes]
            stores.append(pltpu.make_async_copy(total.at[here], out.at[here], sem.at[len(stores)]))
            stores[-1].start()
    loss_ref[0] = jnp.sum(sum(loss[...] for loss in losses)) * (1.0 / count)
    for copy in stores:
        copy.wait()


def finish_sums(groups, losses, length, count):
    width, lanes = groups[0][0][1].shape[1], 128
    smem, anywhere, vmem = (pl.BlockSpec(memory_space=m) for m in (pltpu.SMEM, pl.ANY, pltpu.VMEM))
    flat = [*losses, *(part for group in groups for _, part in group)]
    shape = (length, width // lanes, lanes)
    loss, *outs = pl.pallas_call(
        functools.partial(
            finish_kernel, [[start for start, _ in group] for group in groups], len(losses), count
        ),
        in_specs=[vmem] * len(flat),
        out_specs=[smem] + [anywhere] * len(groups),
        out_shape=[jax.ShapeDtypeStruct((1,), jnp.float32)] + [jax.ShapeDtypeStruct(shape, jnp.float32)] * len(groups),
        scratch_shapes=[pltpu.VMEM(shape, jnp.float32)] * len(groups)
        + [pltpu.SemaphoreType.DMA((len(groups) * (length // 64),))],
        cost_estimate=pl.CostEstimate(flops=6 * length * width, bytes_accessed=20 * length * width, transcendentals=0),
        compiler_params=pltpu.CompilerParams(vmem_limit_bytes=16 << 20),
    )(*[pltpu.with_memory_space_constraint(x, pltpu.VMEM) for x in flat])
    return [loss, *(out.reshape(length, 1, width) for out in outs)]


def step(states, goals, pos_offset, neg_blocks):
    size = lax.axis_size(AXIS)
    length, width = states.shape[0], states.shape[2]
    half = length // 2
    high = size // 2
    inner = []
    bit = size // 4
    while bit > 1:
        inner.append(bit)
        bit //= 2
    across = high ^ (high >> 1)
    blocks = subsets(inner)
    n_block = len(blocks)
    row_xors, col_xors = [0, across], [x ^ side for x in blocks for side in (0, 1)]
    n_row, n_col = len(row_xors) * length, len(col_xors) * length
    last = n_col - 2 * length
    state, goal = states.reshape(length, width), goals.reshape(length, width)
    own = lax.axis_index(AXIS).astype(jnp.int32).reshape(1)

    def outer(i):
        return (i & across) in (0, across)

    mine = [goal]
    for bit in inner:
        mine = mine + [swap(block, bit, size) for block in mine]
    side = [swap(block, 1, size) for block in mine]
    cols = {2 * k * length + p: b for k in range(n_block) for p, b in ((0, mine[k]), (length, side[k]))}
    pair_in = swap(state, across, size, lambda i: not outer(i))
    pair = pair_in + swap(state, across, size, outer)
    table = counts(pos_offset, neg_blocks, size)
    tables = [table, swap(table, across, size)]

    fixed = dict(
        row_xors=row_xors, col_xors=col_xors,
        row_chunks=tuple((k * length, length, k, 0) for k in range(len(row_xors))),
        col_chunks=tuple((k * length, length, k, 0) for k in range(len(col_xors))),
    )

    def arrived(start, end):
        return {p: c for p, c in cols.items() if start <= p < end}

    loss_a, held, _, _ = phase(
        own, tables[:1], {0: state}, arrived(0, 2 * length), None, new=[(0, length, 0, 2 * length)], **fixed
    )
    loss_b, held, _, _ = phase(
        own, tables[:1], {}, arrived(2 * length, last), held, new=[(0, length, 2 * length, last)], **fixed
    )
    loss_c, held, _, _ = phase(own, tables, {length: pair}, {}, held, new=[(length, n_row, 0, last)], **fixed)
    sides, own_sums = {}, {}

    def goal_phase(which, tables, cols, held, new, rows=()):
        pieces = [[(p * length, (p + 1) * length)] for k in which for p in (2 * k + 1, 2 * k)]
        loss, held, row_outs, outs = phase(
            own, tables, {}, cols, held, new=new, row_outs=rows, col_outs=pieces,
            dtypes=[jnp.float32] * len(rows) + [jnp.bfloat16, jnp.float32] * len(which), **fixed,
        )
        sides.update(zip(which, outs[0::2]))
        own_sums.update(zip(which, outs[1::2]))
        return loss, held, row_outs

    top = n_block // 2
    loss_d, held, _ = goal_phase(
        list(range(n_block - 1, top, -1)), tables, arrived(last, n_col), held, [(0, n_row, last, n_col)]
    )
    loss = loss_a + loss_b + loss_c + loss_d
    loss = loss + swap(loss, 1, size)
    _, _, (pair_part,), _ = phase(own, [], {}, {}, held, row_outs=[[(length, n_row)]], **fixed)

    back_pair = swap(pair_part, across, size)
    goal_phase([top], [], {}, held, ())
    _, _, (own_part,) = goal_phase(list(range(top)), [], {}, held, (), rows=[[(0, length)]])
    cross = {k: swap(part, 1, size) for k, part in sides.items()}
    for s in reversed(range(len(inner))):
        loss = loss + swap(loss, inner[s], size)
    losses = [loss, swap(loss, across, size)]
    addends = {k: [(own_sums[k], 0), (cross[k], 0)] for k in range(n_block)}
    halves = {(k, o): [] for k in range(n_block) for o in (0, half)}
    for s in reversed(range(len(inner))):
        for k in reversed(range(1 << s, 2 << s)):
            to = k - (1 << s)
            if to == 0 and s == len(inner) - 1:
                whole = add(length, *addends[k])
                addends[to].append((swap(whole, inner[s], size), 0))
                continue
            for o in (0, half):
                piece = add(half, *[(b, o) for b, _ in addends[k]], *[(b, 0) for b in halves[k, o]])
                halves[to, o].append(swap(piece, inner[s], size))
    goal_parts = [(0, block) for block, _ in addends[0]] + [(o, b) for o in (0, half) for b in halves[0, o]]
    loss_mean, grad_states, grad_goals = finish_sums(
        [[(0, own_part), (0, back_pair)], goal_parts], losses, length, size * length
    )
    return (loss_mean, grad_states, grad_goals)


def solution(mesh):
    spec = P("tm", "groups", None)
    return jax.shard_map(
        step,
        mesh=mesh,
        in_specs=(spec,) * 4,
        out_specs=(P("groups"), spec, spec),
        check_vma=False,
    )
```

```python
import functools
import math

import jax
import jax.numpy as jnp
from jax import lax
from jax.experimental import pallas as pl
from jax.experimental.pallas import tpu as pltpu
from jax.sharding import PartitionSpec as P


AXIS = "tm"


def swap(value, offset, size, only=lambda i: True):
    return lax.ppermute(value, AXIS, [(i, i ^ offset) for i in range(size) if only(i)])


def subsets(bits):
    found = [0]
    for bit in bits:
        found = found + [offset ^ bit for offset in found]
    return found


def fold(part, op):
    pieces = [part[k : k + 8] for k in range(0, part.shape[0], 8)]
    while len(pieces) > 1:
        pieces = [op(*pieces[k : k + 2]) if k + 1 < len(pieces) else pieces[k] for k in range(0, len(pieces), 2)]
    return pieces[0]


def tile_kernel(plan, own_ref, *refs):
    n_new = len(plan["row_places"]) + len(plan["col_places"])
    tables, refs = refs[: plan["n_tables"]], refs[plan["n_tables"] :]
    arrived, refs = refs[:n_new], refs[n_new:]
    if plan["aliased"] or not plan["new"]:
        held, refs = refs[:3], refs[3:]
    if plan["new"]:
        loss_ref, held, refs = refs[0], refs[1:4], refs[4:]
    rows, cols, coeff = held
    row_out, refs = refs[: len(plan["row_outs"])], refs[len(plan["row_outs"]) :]
    col_out, (fresh, sem) = refs[: len(plan["col_outs"])], refs[len(plan["col_outs"]) :]
    width = rows.shape[1]
    inv_root = 1.0 / math.sqrt(width)
    size = tables[0].shape[0] // 2 if tables else 0

    targets = [rows.at[pl.ds(p, r.shape[0])] for p, r in zip(plan["row_places"], arrived)]
    targets += [cols.at[pl.ds(p, r.shape[0])] for p, r in zip(plan["col_places"], arrived[len(targets) :])]
    loads = [pltpu.make_async_copy(s, t, sem.at[k]) for k, (s, t) in enumerate(zip(arrived, targets))]
    for copy in loads:
        copy.start()
    for copy in loads:
        copy.wait()

    if plan["new"]:
        own = own_ref[0]
        loss = jnp.zeros((8, 128), jnp.float32)
        at, kept = 0, []
        for r0, r1, c0, c1 in plan["new"]:
            buffer = fresh.at[pl.ds(at, c1 - c0), pl.ds(0, r1 - r0)]
            at += c1 - c0
            kept.append((buffer, coeff.at[pl.ds(c0, c1 - c0), pl.ds(r0, r1 - r0)]))
            dots = lax.dot_general(
                cols[c0:c1, :], rows[r0:r1, :], (((1,), (1,)), ((), ())), preferred_element_type=jnp.float32
            )
            for cp, cl, j, c_off in plan["col_chunks"]:
                if cp < c0 or cp >= c1:
                    continue
                target = own ^ plan["col_xors"][j]
                for rp, rl, i, r_off in plan["row_chunks"]:
                    if rp < r0 or rp >= r1:
                        continue
                    raw = dots[cp - c0 : cp - c0 + cl, rp - r0 : rp - r0 + rl]
                    pos, neg = tables[i][target], tables[i][size + target]
                    decay = jnp.exp2(jnp.abs(raw) * (-inv_root * math.log2(math.e)))
                    whole = 1.0 + decay
                    large = pl.reciprocal(whole)
                    up = raw >= 0.0
                    above = jnp.maximum(raw, 0.0)
                    if plan["row_xors"][i] == plan["col_xors"][j]:
                        later = lax.broadcasted_iota(jnp.int32, raw.shape, 0) + c_off > (
                            lax.broadcasted_iota(jnp.int32, raw.shape, 1) + r_off
                        )
                        pos = jnp.where(later, pos, 0.0)
                        soft = jnp.log(whole)
                        above, below = above * inv_root, (above - raw) * inv_root
                        part = fold(pos * (below + soft) + neg * (above + soft), jnp.add)
                    else:
                        over, total = fold(above, jnp.add) * inv_root, fold(raw, jnp.add) * inv_root
                        part = neg * over + pos * (over - total)
                        part = part + (pos + neg) * jnp.log(fold(whole, jnp.multiply))
                    gain, drop = neg * inv_root, pos * inv_root
                    values = (jnp.where(up, gain, -drop) + jnp.where(up, -drop, gain) * decay) * large
                    for k in range(0, part.shape[1], 128):
                        loss = loss + part[:, k : k + 128]
                    buffer[cp - c0 : cp - c0 + cl, rp - r0 : rp - r0 + rl] = values.astype(jnp.bfloat16)
        loss_ref[...] = loss
        copies = [pltpu.make_async_copy(s, t, sem.at[n_new + k]) for k, (s, t) in enumerate(kept)]
        for copy in copies:
            copy.start()
        for copy in copies:
            copy.wait()

    def finish(outs, pieces, compute):
        if not outs:
            return
        low, high = min(p[0] for out in pieces for p in out), max(p[1] for out in pieces for p in out)
        for base in range(low, high, plan["step"]):
            top = min(high, base + plan["step"])
            value = compute(base, top)
            for out, parts in zip(outs, pieces):
                at = 0
                for p0, p1 in parts:
                    a, b = max(p0, base), min(p1, top)
                    if a < b:
                        out[at + a - p0 : at + b - p0, :] = value[a - base : b - base].astype(out.dtype)
                    at += p1 - p0

    finish(row_out, plan["row_outs"], lambda a, b: lax.dot_general(
        coeff[:, a:b], cols[...], (((0,), (0,)), ((), ())), preferred_element_type=jnp.float32))
    finish(col_out, plan["col_outs"], lambda a, b: jnp.dot(
        coeff[a:b, :], rows[...], preferred_element_type=jnp.float32))


def phase(own, tables, rows, cols, held, row_chunks, col_chunks, row_xors, col_xors, new=(), row_outs=(),
          col_outs=(), dtypes=None):
    n_row, n_col = (sum(c[1] for c in chunks) for chunks in (row_chunks, col_chunks))
    tables = tables if new else []
    width = next(iter(rows.values())).shape[1] if rows else held[0].shape[1]
    plan = dict(
        row_chunks=row_chunks, col_chunks=col_chunks, row_xors=row_xors, col_xors=col_xors, n_tables=len(tables),
        row_places=list(rows), col_places=list(cols), aliased=held is not None, new=new, row_outs=row_outs,
        col_outs=col_outs, step=512,
    )
    smem, anywhere, vmem = (pl.BlockSpec(memory_space=m) for m in (pltpu.SMEM, pl.ANY, pltpu.VMEM))
    args = [own, *tables, *rows.values(), *cols.values()]
    in_specs = [smem] * (1 + len(tables)) + [anywhere] * (len(rows) + len(cols))
    out_shape, aliases = [], {}
    if new:
        out_shape.append(pltpu.VMEM((8, 128), jnp.float32))
        if held is not None:
            aliases = {len(args) + k: 1 + k for k in range(3)}
        out_shape += [
            pltpu.VMEM(shape, jnp.bfloat16) for shape in ((n_row, width), (n_col, width), (n_col, n_row))
        ]
    if held is not None:
        args += [pltpu.with_memory_space_constraint(x, pltpu.VMEM) for x in held]
        in_specs += [vmem] * 3
    outs = (*row_outs, *col_outs)
    lengths = [sum(b - a for a, b in out) for out in outs]
    dtypes = dtypes or [jnp.bfloat16] * len(lengths)
    out_shape += [pltpu.VMEM((n, width), dtype) for n, dtype in zip(lengths, dtypes)]
    row_total, col_total = sum(lengths[: len(row_outs)]), sum(lengths[len(row_outs) :])
    area = sum((r1 - r0) * (c1 - c0) for r0, r1, c0, c1 in new)
    flops = 2 * width * (area + row_total * n_col + col_total * n_row)
    outs = list(
        pl.pallas_call(
            functools.partial(tile_kernel, plan),
            in_specs=in_specs,
            out_specs=[vmem] * len(out_shape),
            out_shape=out_shape,
            input_output_aliases=aliases,
            scratch_shapes=[
                pltpu.VMEM(
                    (max(16, sum(c1 - c0 for _, _, c0, c1 in new)), max([128] + [r1 - r0 for r0, r1, _, _ in new])),
                    jnp.bfloat16,
                ),
                pltpu.SemaphoreType.DMA((max(1, len(rows) + len(cols) + len(new)),)),
            ],
            cost_estimate=pl.CostEstimate(flops=flops, bytes_accessed=4 * width * width, transcendentals=2 * area),
            compiler_params=pltpu.CompilerParams(vmem_limit_bytes=20 << 20),
        )(*args)
    )
    loss = outs.pop(0) if new else None
    if new:
        held, outs = outs[:3], outs[3:]
    return loss, held, outs[: len(row_outs)], outs[len(row_outs) :]


def counts(pos_offset, neg_blocks, size):
    blocks = jnp.arange(size, dtype=jnp.int32)
    target = lax.axis_index(AXIS).astype(jnp.int32) + pos_offset.reshape(-1)
    pos = jnp.sum((target[:, None] == blocks).astype(jnp.float32), axis=0)
    neg = jnp.sum((neg_blocks.reshape(-1)[:, None] == blocks).astype(jnp.float32), axis=0)
    return jnp.concatenate([pos, neg])


def add_kernel(starts, *refs):
    *parts, out = refs
    out[...] = sum(
        part[start : start + out.shape[0], :].astype(jnp.float32) for start, part in zip(starts, parts)
    ).astype(out.dtype)


def add(rows, *parts):
    vmem = pl.BlockSpec(memory_space=pltpu.VMEM)
    width = parts[0][0].shape[1]
    return pl.pallas_call(
        functools.partial(add_kernel, [start for _, start in parts]),
        in_specs=[vmem] * len(parts),
        out_specs=vmem,
        out_shape=pltpu.VMEM((rows, width), jnp.bfloat16),
        cost_estimate=pl.CostEstimate(
            flops=rows * width * len(parts), bytes_accessed=4 * rows * width, transcendentals=0
        ),
        compiler_params=pltpu.CompilerParams(vmem_limit_bytes=4 << 20),
    )(*[pltpu.with_memory_space_constraint(part, pltpu.VMEM) for part, _ in parts])


def finish_kernel(groups, n_loss, count, *refs):
    n_in = sum(len(group) for group in groups)
    losses, ins, refs = refs[:n_loss], list(refs[n_loss : n_loss + n_in]), refs[n_loss + n_in :]
    loss_ref, outs, totals, sem = refs[0], refs[1 : 1 + len(groups)], refs[1 + len(groups) : -1], refs[-1]
    n, stores = 64, []
    for starts, out, total in zip(groups, outs, totals):
        parts = [(start, ins.pop(0)) for start in starts]
        for r in range(0, out.shape[0], n):
            here = pl.ds(r, n)
            value = sum(
                part[r - start : r - start + n, :].astype(jnp.float32)
                for start, part in parts
                if start <= r < start + part.shape[0]
            )
            total[here, :] = value
            stores.append(pltpu.make_async_copy(total.at[here], out.at[here, 0, :], sem.at[len(stores)]))
            stores[-1].start()
    loss_ref[0] = jnp.sum(sum(loss[...] for loss in losses)) * (1.0 / count)
    for copy in stores:
        copy.wait()


def finish_sums(groups, losses, length, count):
    width = groups[0][0][1].shape[1]
    smem, anywhere, vmem = (pl.BlockSpec(memory_space=m) for m in (pltpu.SMEM, pl.ANY, pltpu.VMEM))
    flat = [*losses, *(part for group in groups for _, part in group)]
    shape = (length, 1, width)
    loss, *outs = pl.pallas_call(
        functools.partial(
            finish_kernel, [[start for start, _ in group] for group in groups], len(losses), count
        ),
        in_specs=[vmem] * len(flat),
        out_specs=[smem] + [anywhere] * len(groups),
        out_shape=[jax.ShapeDtypeStruct((1,), jnp.float32)] + [jax.ShapeDtypeStruct(shape, jnp.float32)] * len(groups),
        scratch_shapes=[pltpu.VMEM((length, width), jnp.float32)] * len(groups)
        + [pltpu.SemaphoreType.DMA((len(groups) * (length // 64),))],
        cost_estimate=pl.CostEstimate(flops=6 * length * width, bytes_accessed=20 * length * width, transcendentals=0),
        compiler_params=pltpu.CompilerParams(vmem_limit_bytes=16 << 20),
    )(*[pltpu.with_memory_space_constraint(x, pltpu.VMEM) for x in flat])
    return [loss, *outs]


def step(states, goals, pos_offset, neg_blocks):
    size = lax.axis_size(AXIS)
    length, width = states.shape[0], states.shape[2]
    half = length // 2
    high = size // 2
    inner = []
    bit = size // 4
    while bit > 1:
        inner.append(bit)
        bit //= 2
    across = high ^ (high >> 1)
    blocks = subsets(inner)
    n_block = len(blocks)
    row_xors, col_xors = [0, across], [x ^ side for x in blocks for side in (0, 1)]
    n_row, n_col = len(row_xors) * length, len(col_xors) * length
    last = n_col - 2 * length
    state, goal = states.reshape(length, width), goals.reshape(length, width)
    own = lax.axis_index(AXIS).astype(jnp.int32).reshape(1)

    def outer(i):
        return (i & across) in (0, across)

    mine = [goal]
    for bit in inner:
        mine = mine + [swap(block, bit, size) for block in mine]
    side = [swap(block, 1, size) for block in mine]
    cols = {2 * k * length + p: b for k in range(n_block) for p, b in ((0, mine[k]), (length, side[k]))}
    pair_in = swap(state, across, size, lambda i: not outer(i))
    pair = pair_in + swap(state, across, size, outer)
    table = counts(pos_offset, neg_blocks, size)
    tables = [table, swap(table, across, size)]

    fixed = dict(
        row_xors=row_xors, col_xors=col_xors,
        row_chunks=tuple((k * length, length, k, 0) for k in range(len(row_xors))),
        col_chunks=tuple((k * length, length, k, 0) for k in range(len(col_xors))),
    )

    def arrived(start, end):
        return {p: c for p, c in cols.items() if start <= p < end}

    loss_a, held, _, _ = phase(
        own, tables[:1], {0: state}, arrived(0, 2 * length), None, new=[(0, length, 0, 2 * length)], **fixed
    )
    loss_b, held, _, _ = phase(
        own, tables[:1], {}, arrived(2 * length, last), held, new=[(0, length, 2 * length, last)], **fixed
    )
    loss_c, held, _, _ = phase(own, tables, {length: pair}, {}, held, new=[(length, n_row, 0, last)], **fixed)
    sides, own_sums = {}, {}

    def goal_phase(which, tables, cols, held, new, rows=()):
        pieces = [[(p * length, (p + 1) * length)] for k in which for p in (2 * k + 1, 2 * k)]
        loss, held, row_outs, outs = phase(
            own, tables, {}, cols, held, new=new, row_outs=rows, col_outs=pieces,
            dtypes=[jnp.float32] * len(rows) + [jnp.bfloat16, jnp.float32] * len(which), **fixed,
        )
        sides.update(zip(which, outs[0::2]))
        own_sums.update(zip(which, outs[1::2]))
        return loss, held, row_outs

    top = n_block // 2
    loss_d, held, _ = goal_phase(
        list(range(n_block - 1, top, -1)), tables, arrived(last, n_col), held, [(0, n_row, last, n_col)]
    )
    loss = loss_a + loss_b + loss_c + loss_d
    _, _, (pair_part,), _ = phase(own, [], {}, {}, held, row_outs=[[(length, n_row)]], **fixed)

    back_pair = swap(pair_part, across, size)
    goal_phase([top], [], {}, held, ())
    _, _, (own_part,) = goal_phase(list(range(top)), [], {}, held, (), rows=[[(0, length)]])
    cross = {k: swap(part, 1, size) for k, part in sides.items()}
    for s in reversed(range(len(inner))):
        loss = loss + swap(loss, inner[s], size)
        if s == len(inner) - 1:
            loss = loss + swap(loss, 1, size)
    losses = [loss, swap(loss, across, size)]
    addends = {k: [(own_sums[k], 0), (cross[k], 0)] for k in range(n_block)}
    halves = {(k, o): [] for k in range(n_block) for o in (0, half)}
    for s in reversed(range(len(inner))):
        for k in reversed(range(1 << s, 2 << s)):
            to = k - (1 << s)
            if to == 0 and s == len(inner) - 1:
                whole = add(length, *addends[k])
                addends[to].append((swap(whole, inner[s], size), 0))
                continue
            for o in (0, half):
                piece = add(half, *[(b, o) for b, _ in addends[k]], *[(b, 0) for b in halves[k, o]])
                halves[to, o].append(swap(piece, inner[s], size))
    goal_parts = [(0, block) for block, _ in addends[0]] + [(o, b) for o in (0, half) for b in halves[0, o]]
    _, grad_states = finish_sums([[(0, own_part), (0, back_pair)]], losses[:1], length, size * length)
    loss_mean, grad_goals = finish_sums([goal_parts], losses, length, size * length)
    return (loss_mean, grad_states, grad_goals)


def solution(mesh):
    spec = P("tm", "groups", None)
    return jax.shard_map(
        step,
        mesh=mesh,
        in_specs=(spec,) * 4,
        out_specs=(P("groups"), spec, spec),
        check_vma=False,
    )
```

```python
import functools
import math

import jax
import jax.numpy as jnp
from jax import lax
from jax.experimental import pallas as pl
from jax.experimental.pallas import tpu as pltpu
from jax.sharding import PartitionSpec as P


AXIS = "tm"


def swap(value, offset, size, only=lambda i: True):
    return lax.ppermute(value, AXIS, [(i, i ^ offset) for i in range(size) if only(i)])


def subsets(bits):
    found = [0]
    for bit in bits:
        found = found + [offset ^ bit for offset in found]
    return found


def fold(part, op):
    pieces = [part[k : k + 8] for k in range(0, part.shape[0], 8)]
    while len(pieces) > 1:
        pieces = [op(*pieces[k : k + 2]) if k + 1 < len(pieces) else pieces[k] for k in range(0, len(pieces), 2)]
    return pieces[0]


def tile_kernel(plan, own_ref, *refs):
    n_new = len(plan["row_places"]) + len(plan["col_places"])
    tables, refs = refs[: plan["n_tables"]], refs[plan["n_tables"] :]
    arrived, refs = refs[:n_new], refs[n_new:]
    if plan["aliased"] or not plan["new"]:
        held, refs = refs[:3], refs[3:]
    if plan["new"]:
        loss_ref, held, refs = refs[0], refs[1:4], refs[4:]
    rows, cols, coeff = held
    row_out, refs = refs[: len(plan["row_outs"])], refs[len(plan["row_outs"]) :]
    col_out, (fresh, sem) = refs[: len(plan["col_outs"])], refs[len(plan["col_outs"]) :]
    width = rows.shape[1]
    inv_root = 1.0 / math.sqrt(width)
    size = tables[0].shape[0] // 2 if tables else 0

    targets = [rows.at[pl.ds(p, r.shape[0])] for p, r in zip(plan["row_places"], arrived)]
    targets += [cols.at[pl.ds(p, r.shape[0])] for p, r in zip(plan["col_places"], arrived[len(targets) :])]
    loads = [pltpu.make_async_copy(s, t, sem.at[k]) for k, (s, t) in enumerate(zip(arrived, targets))]
    for copy in loads:
        copy.start()
    for copy in loads:
        copy.wait()

    if plan["new"]:
        own = own_ref[0]
        loss = jnp.zeros((8, 128), jnp.float32)
        at, kept = 0, []
        for r0, r1, c0, c1 in plan["new"]:
            buffer = fresh.at[pl.ds(at, c1 - c0), pl.ds(0, r1 - r0)]
            at += c1 - c0
            kept.append((buffer, coeff.at[pl.ds(c0, c1 - c0), pl.ds(r0, r1 - r0)]))
            dots = lax.dot_general(
                cols[c0:c1, :], rows[r0:r1, :], (((1,), (1,)), ((), ())), preferred_element_type=jnp.float32
            )
            for cp, cl, j, c_off in plan["col_chunks"]:
                if cp < c0 or cp >= c1:
                    continue
                target = own ^ plan["col_xors"][j]
                for rp, rl, i, r_off in plan["row_chunks"]:
                    if rp < r0 or rp >= r1:
                        continue
                    raw = dots[cp - c0 : cp - c0 + cl, rp - r0 : rp - r0 + rl]
                    pos, neg = tables[i][target], tables[i][size + target]
                    decay = jnp.exp2(jnp.abs(raw) * (-inv_root * math.log2(math.e)))
                    whole = 1.0 + decay
                    large = pl.reciprocal(whole)
                    up = raw >= 0.0
                    above = jnp.maximum(raw, 0.0)
                    if plan["row_xors"][i] == plan["col_xors"][j]:
                        later = lax.broadcasted_iota(jnp.int32, raw.shape, 0) + c_off > (
                            lax.broadcasted_iota(jnp.int32, raw.shape, 1) + r_off
                        )
                        pos = jnp.where(later, pos, 0.0)
                        soft = jnp.log(whole)
                        above, below = above * inv_root, (above - raw) * inv_root
                        part = fold(pos * (below + soft) + neg * (above + soft), jnp.add)
                    else:
                        over, total = fold(above, jnp.add) * inv_root, fold(raw, jnp.add) * inv_root
                        part = neg * over + pos * (over - total)
                        part = part + (pos + neg) * jnp.log(fold(whole, jnp.multiply))
                    gain, drop = neg * inv_root, pos * inv_root
                    values = (jnp.where(up, gain, -drop) + jnp.where(up, -drop, gain) * decay) * large
                    for k in range(0, part.shape[1], 128):
                        loss = loss + part[:, k : k + 128]
                    buffer[cp - c0 : cp - c0 + cl, rp - r0 : rp - r0 + rl] = values.astype(jnp.bfloat16)
        loss_ref[...] = loss
        copies = [pltpu.make_async_copy(s, t, sem.at[n_new + k]) for k, (s, t) in enumerate(kept)]
        for copy in copies:
            copy.start()
        for copy in copies:
            copy.wait()

    def finish(outs, pieces, compute):
        if not outs:
            return
        low, high = min(p[0] for out in pieces for p in out), max(p[1] for out in pieces for p in out)
        for base in range(low, high, plan["step"]):
            top = min(high, base + plan["step"])
            value = compute(base, top)
            for out, parts in zip(outs, pieces):
                at = 0
                for p0, p1 in parts:
                    a, b = max(p0, base), min(p1, top)
                    if a < b:
                        out[at + a - p0 : at + b - p0, :] = value[a - base : b - base].astype(out.dtype)
                    at += p1 - p0

    finish(row_out, plan["row_outs"], lambda a, b: lax.dot_general(
        coeff[:, a:b], cols[...], (((0,), (0,)), ((), ())), preferred_element_type=jnp.float32))
    finish(col_out, plan["col_outs"], lambda a, b: jnp.dot(
        coeff[a:b, :], rows[...], preferred_element_type=jnp.float32))


def phase(own, tables, rows, cols, held, row_chunks, col_chunks, row_xors, col_xors, new=(), row_outs=(),
          col_outs=(), dtypes=None):
    n_row, n_col = (sum(c[1] for c in chunks) for chunks in (row_chunks, col_chunks))
    tables = tables if new else []
    width = next(iter(rows.values())).shape[1] if rows else held[0].shape[1]
    plan = dict(
        row_chunks=row_chunks, col_chunks=col_chunks, row_xors=row_xors, col_xors=col_xors, n_tables=len(tables),
        row_places=list(rows), col_places=list(cols), aliased=held is not None, new=new, row_outs=row_outs,
        col_outs=col_outs, step=512,
    )
    smem, anywhere, vmem = (pl.BlockSpec(memory_space=m) for m in (pltpu.SMEM, pl.ANY, pltpu.VMEM))
    args = [own, *tables, *rows.values(), *cols.values()]
    in_specs = [smem] * (1 + len(tables)) + [anywhere] * (len(rows) + len(cols))
    out_shape, aliases = [], {}
    if new:
        out_shape.append(pltpu.VMEM((8, 128), jnp.float32))
        if held is not None:
            aliases = {len(args) + k: 1 + k for k in range(3)}
        out_shape += [
            pltpu.VMEM(shape, jnp.bfloat16) for shape in ((n_row, width), (n_col, width), (n_col, n_row))
        ]
    if held is not None:
        args += [pltpu.with_memory_space_constraint(x, pltpu.VMEM) for x in held]
        in_specs += [vmem] * 3
    outs = (*row_outs, *col_outs)
    lengths = [sum(b - a for a, b in out) for out in outs]
    dtypes = dtypes or [jnp.bfloat16] * len(lengths)
    out_shape += [pltpu.VMEM((n, width), dtype) for n, dtype in zip(lengths, dtypes)]
    row_total, col_total = sum(lengths[: len(row_outs)]), sum(lengths[len(row_outs) :])
    area = sum((r1 - r0) * (c1 - c0) for r0, r1, c0, c1 in new)
    flops = 2 * width * (area + row_total * n_col + col_total * n_row)
    outs = list(
        pl.pallas_call(
            functools.partial(tile_kernel, plan),
            in_specs=in_specs,
            out_specs=[vmem] * len(out_shape),
            out_shape=out_shape,
            input_output_aliases=aliases,
            scratch_shapes=[
                pltpu.VMEM(
                    (max(16, sum(c1 - c0 for _, _, c0, c1 in new)), max([128] + [r1 - r0 for r0, r1, _, _ in new])),
                    jnp.bfloat16,
                ),
                pltpu.SemaphoreType.DMA((max(1, len(rows) + len(cols) + len(new)),)),
            ],
            cost_estimate=pl.CostEstimate(flops=flops, bytes_accessed=4 * width * width, transcendentals=2 * area),
            compiler_params=pltpu.CompilerParams(vmem_limit_bytes=20 << 20),
        )(*args)
    )
    loss = outs.pop(0) if new else None
    if new:
        held, outs = outs[:3], outs[3:]
    return loss, held, outs[: len(row_outs)], outs[len(row_outs) :]


def counts(pos_offset, neg_blocks, size):
    blocks = jnp.arange(size, dtype=jnp.int32)
    target = lax.axis_index(AXIS).astype(jnp.int32) + pos_offset.reshape(-1)
    pos = jnp.sum((target[:, None] == blocks).astype(jnp.float32), axis=0)
    neg = jnp.sum((neg_blocks.reshape(-1)[:, None] == blocks).astype(jnp.float32), axis=0)
    return jnp.concatenate([pos, neg])


def add_kernel(starts, *refs):
    *parts, out = refs
    out[...] = sum(
        part[start : start + out.shape[0], :].astype(jnp.float32) for start, part in zip(starts, parts)
    ).astype(out.dtype)


def add(rows, *parts):
    vmem = pl.BlockSpec(memory_space=pltpu.VMEM)
    width = parts[0][0].shape[1]
    return pl.pallas_call(
        functools.partial(add_kernel, [start for _, start in parts]),
        in_specs=[vmem] * len(parts),
        out_specs=vmem,
        out_shape=pltpu.VMEM((rows, width), jnp.bfloat16),
        cost_estimate=pl.CostEstimate(
            flops=rows * width * len(parts), bytes_accessed=4 * rows * width, transcendentals=0
        ),
        compiler_params=pltpu.CompilerParams(vmem_limit_bytes=4 << 20),
    )(*[pltpu.with_memory_space_constraint(part, pltpu.VMEM) for part, _ in parts])


def finish_kernel(n_loss, firsts, in_place, count, start, *refs):
    n_part = len(firsts)
    losses, parts, refs = refs[:n_loss], refs[n_loss : n_loss + n_part], refs[n_loss + n_part + in_place :]
    *outs, total, sem = refs
    if n_loss:
        outs[-2][0] = jnp.sum(sum(loss[...] for loss in losses)) * (1.0 / count)
    rows, n, stores = total.shape[0], 64, []
    for r in range(0, rows, n):
        here = pl.ds(r, n)
        total[here, :] = sum(part[f + r : f + r + n, :].astype(jnp.float32) for f, part in zip(firsts, parts))
        there = outs[-1].at[pl.ds(start + r, n), 0, :]
        stores.append(pltpu.make_async_copy(total.at[here], there, sem.at[len(stores)]))
        stores[-1].start()
    for copy in stores:
        copy.wait()


def finish_rows(rows, parts, length, start=0, into=None, losses=(), count=1):
    width = parts[0][0].shape[1]
    smem, anywhere, vmem = (pl.BlockSpec(memory_space=m) for m in (pltpu.SMEM, pl.ANY, pltpu.VMEM))
    held = [pltpu.with_memory_space_constraint(x, pltpu.VMEM) for x in (*losses, *(block for block, _ in parts))]
    out_shape = [jax.ShapeDtypeStruct((length, 1, width), jnp.float32)]
    out_specs = [anywhere]
    if losses:
        out_shape, out_specs = [jax.ShapeDtypeStruct((1,), jnp.float32), *out_shape], [smem, anywhere]
    in_place = into is not None
    return pl.pallas_call(
        functools.partial(finish_kernel, len(losses), [first for _, first in parts], in_place, count, start),
        in_specs=[vmem] * len(held) + [anywhere] * in_place,
        out_specs=out_specs,
        out_shape=out_shape,
        input_output_aliases={len(held): len(out_shape) - 1} if in_place else {},
        scratch_shapes=[pltpu.VMEM((rows, width), jnp.float32), pltpu.SemaphoreType.DMA((rows // 64,))],
        cost_estimate=pl.CostEstimate(flops=4 * rows * width, bytes_accessed=14 * rows * width, transcendentals=0),
        compiler_params=pltpu.CompilerParams(vmem_limit_bytes=8 << 20),
    )(*held, *([into] if in_place else []))


def step(states, goals, pos_offset, neg_blocks):
    size = lax.axis_size(AXIS)
    length, width = states.shape[0], states.shape[2]
    half = length // 2
    high = size // 2
    inner = []
    bit = size // 4
    while bit > 1:
        inner.append(bit)
        bit //= 2
    across = high ^ (high >> 1)
    blocks = subsets(inner)
    n_block = len(blocks)
    row_xors, col_xors = [0, across], [x ^ side for x in blocks for side in (0, 1)]
    n_row, n_col = len(row_xors) * length, len(col_xors) * length
    last = n_col - 2 * length
    state, goal = states.reshape(length, width), goals.reshape(length, width)
    own = lax.axis_index(AXIS).astype(jnp.int32).reshape(1)

    def outer(i):
        return (i & across) in (0, across)

    mine = [goal]
    for bit in inner:
        mine = mine + [swap(block, bit, size) for block in mine]
    side = [swap(block, 1, size) for block in mine]
    cols = {2 * k * length + p: b for k in range(n_block) for p, b in ((0, mine[k]), (length, side[k]))}
    pair_in = swap(state, across, size, lambda i: not outer(i))
    pair = pair_in + swap(state, across, size, outer)
    table = counts(pos_offset, neg_blocks, size)
    tables = [table, swap(table, across, size)]

    fixed = dict(
        row_xors=row_xors, col_xors=col_xors,
        row_chunks=tuple((k * length, length, k, 0) for k in range(len(row_xors))),
        col_chunks=tuple((k * length, length, k, 0) for k in range(len(col_xors))),
    )

    def arrived(start, end):
        return {p: c for p, c in cols.items() if start <= p < end}

    loss_a, held, _, _ = phase(
        own, tables[:1], {0: state}, arrived(0, length), None, new=[(0, length, 0, length)], **fixed
    )
    loss_b, held, _, _ = phase(
        own, tables[:1], {}, arrived(length, last), held, new=[(0, length, length, last)], **fixed
    )
    loss_c, held, _, _ = phase(own, tables, {length: pair}, {}, held, new=[(length, n_row, 0, last)], **fixed)
    sides, own_sums = {}, {}

    def goal_phase(which, tables, cols, held, new, rows=()):
        pieces = [[(p * length, (p + 1) * length)] for k in which for p in (2 * k + 1, 2 * k)]
        loss, held, row_outs, outs = phase(
            own, tables, {}, cols, held, new=new, row_outs=rows, col_outs=pieces,
            dtypes=[jnp.float32] * len(rows) + [jnp.bfloat16, jnp.float32] * len(which), **fixed,
        )
        sides.update(zip(which, outs[0::2]))
        own_sums.update(zip(which, outs[1::2]))
        return loss, held, row_outs

    top = n_block // 2
    loss_d, held, _ = goal_phase(
        list(range(n_block - 1, top, -1)), tables, arrived(last, n_col), held, [(0, n_row, last, n_col)]
    )
    loss = loss_a + loss_b + loss_c + loss_d
    _, _, (pair_part,), _ = phase(own, [], {}, {}, held, row_outs=[[(length, n_row)]], **fixed)

    back_pair = swap(pair_part, across, size)
    goal_phase([top], [], {}, held, ())
    _, _, (own_part,) = goal_phase(list(range(top)), [], {}, held, (), rows=[[(0, length)]])
    cross = {k: swap(part, 1, size) for k, part in sides.items()}
    loss = loss + swap(loss, 1, size)
    for s in reversed(range(len(inner))):
        loss = loss + swap(loss, inner[s], size)
    losses = [loss, swap(loss, across, size)]
    addends = {k: [(own_sums[k], 0), (cross[k], 0)] for k in range(n_block)}
    halves = {(k, o): [] for k in range(n_block) for o in (0, half)}
    for s in reversed(range(len(inner))):
        for k in reversed(range(1 << s, 2 << s)):
            to = k - (1 << s)
            for o in (0, half):
                piece = add(half, *[(b, o) for b, _ in addends[k]], *[(b, 0) for b in halves[k, o]])
                halves[to, o].append(swap(piece, inner[s], size))
    pieces = [[(block, o) for block, _ in addends[0]] + [(block, 0) for block in halves[0, o]] for o in (0, half)]
    (grad_goals,) = finish_rows(half, pieces[0], length)
    loss_mean, grad_states = finish_rows(
        length, [(own_part, 0), (back_pair, 0)], length, losses=losses, count=size * length
    )
    (grad_goals,) = finish_rows(half, pieces[1], length, start=half, into=grad_goals)
    return (loss_mean, grad_states, grad_goals)


def solution(mesh):
    spec = P("tm", "groups", None)
    return jax.shard_map(
        step,
        mesh=mesh,
        in_specs=(spec,) * 4,
        out_specs=(P("groups"), spec, spec),
        check_vma=False,
    )
```

```python
import functools
import math

import jax
import jax.numpy as jnp
from jax import lax
from jax.experimental import pallas as pl
from jax.experimental.pallas import tpu as pltpu
from jax.sharding import PartitionSpec as P


AXIS = "tm"


def swap(value, offset, size, only=lambda i: True):
    return lax.ppermute(value, AXIS, [(i, i ^ offset) for i in range(size) if only(i)])


def subsets(bits):
    found = [0]
    for bit in bits:
        found = found + [offset ^ bit for offset in found]
    return found


def fold(part, op):
    pieces = [part[k : k + 8] for k in range(0, part.shape[0], 8)]
    while len(pieces) > 1:
        pieces = [op(*pieces[k : k + 2]) if k + 1 < len(pieces) else pieces[k] for k in range(0, len(pieces), 2)]
    return pieces[0]


def tile_kernel(plan, own_ref, *refs):
    n_new = len(plan["row_places"]) + len(plan["col_places"])
    tables, refs = refs[: plan["n_tables"]], refs[plan["n_tables"] :]
    arrived, refs = refs[:n_new], refs[n_new:]
    if plan["aliased"] or not plan["new"]:
        held, refs = refs[:3], refs[3:]
    if plan["new"]:
        loss_ref, held, refs = refs[0], refs[1:4], refs[4:]
    rows, cols, coeff = held
    row_out, refs = refs[: len(plan["row_outs"])], refs[len(plan["row_outs"]) :]
    col_out, (fresh, sem) = refs[: len(plan["col_outs"])], refs[len(plan["col_outs"]) :]
    width = rows.shape[1]
    inv_root = 1.0 / math.sqrt(width)
    size = tables[0].shape[0] // 2 if tables else 0

    targets = [rows.at[pl.ds(p, r.shape[0])] for p, r in zip(plan["row_places"], arrived)]
    targets += [cols.at[pl.ds(p, r.shape[0])] for p, r in zip(plan["col_places"], arrived[len(targets) :])]
    loads = [pltpu.make_async_copy(s, t, sem.at[k]) for k, (s, t) in enumerate(zip(arrived, targets))]
    for copy in loads:
        copy.start()
    for copy in loads:
        copy.wait()

    if plan["new"]:
        own = own_ref[0]
        loss = jnp.zeros((8, 128), jnp.float32)
        at, kept = 0, []
        for r0, r1, c0, c1 in plan["new"]:
            buffer = fresh.at[pl.ds(at, c1 - c0), pl.ds(0, r1 - r0)]
            at += c1 - c0
            kept.append((buffer, coeff.at[pl.ds(c0, c1 - c0), pl.ds(r0, r1 - r0)]))
            dots = lax.dot_general(
                cols[c0:c1, :], rows[r0:r1, :], (((1,), (1,)), ((), ())), preferred_element_type=jnp.float32
            )
            for cp, cl, j, c_off in plan["col_chunks"]:
                if cp < c0 or cp >= c1:
                    continue
                target = own ^ plan["col_xors"][j]
                for rp, rl, i, r_off in plan["row_chunks"]:
                    if rp < r0 or rp >= r1:
                        continue
                    raw = dots[cp - c0 : cp - c0 + cl, rp - r0 : rp - r0 + rl]
                    pos, neg = tables[i][target], tables[i][size + target]
                    decay = jnp.exp2(jnp.abs(raw) * (-inv_root * math.log2(math.e)))
                    whole = 1.0 + decay
                    large = pl.reciprocal(whole)
                    up = raw >= 0.0
                    above = jnp.maximum(raw, 0.0)
                    if plan["row_xors"][i] == plan["col_xors"][j]:
                        later = lax.broadcasted_iota(jnp.int32, raw.shape, 0) + c_off > (
                            lax.broadcasted_iota(jnp.int32, raw.shape, 1) + r_off
                        )
                        pos = jnp.where(later, pos, 0.0)
                        soft = jnp.log(whole)
                        above, below = above * inv_root, (above - raw) * inv_root
                        part = fold(pos * (below + soft) + neg * (above + soft), jnp.add)
                    else:
                        over, total = fold(above, jnp.add) * inv_root, fold(raw, jnp.add) * inv_root
                        part = neg * over + pos * (over - total)
                        part = part + (pos + neg) * jnp.log(fold(whole, jnp.multiply))
                    gain, drop = neg * inv_root, pos * inv_root
                    values = (jnp.where(up, gain, -drop) + jnp.where(up, -drop, gain) * decay) * large
                    for k in range(0, part.shape[1], 128):
                        loss = loss + part[:, k : k + 128]
                    buffer[cp - c0 : cp - c0 + cl, rp - r0 : rp - r0 + rl] = values.astype(jnp.bfloat16)
        loss_ref[...] = loss
        copies = [pltpu.make_async_copy(s, t, sem.at[n_new + k]) for k, (s, t) in enumerate(kept)]
        for copy in copies:
            copy.start()
        for copy in copies:
            copy.wait()

    def finish(outs, pieces, compute):
        if not outs:
            return
        low, high = min(p[0] for out in pieces for p in out), max(p[1] for out in pieces for p in out)
        for base in range(low, high, plan["step"]):
            top = min(high, base + plan["step"])
            value = compute(base, top)
            for out, parts in zip(outs, pieces):
                at = 0
                for p0, p1 in parts:
                    a, b = max(p0, base), min(p1, top)
                    if a < b:
                        out[at + a - p0 : at + b - p0, :] = value[a - base : b - base].astype(out.dtype)
                    at += p1 - p0

    finish(row_out, plan["row_outs"], lambda a, b: lax.dot_general(
        coeff[:, a:b], cols[...], (((0,), (0,)), ((), ())), preferred_element_type=jnp.float32))
    finish(col_out, plan["col_outs"], lambda a, b: jnp.dot(
        coeff[a:b, :], rows[...], preferred_element_type=jnp.float32))


def phase(own, tables, rows, cols, held, row_chunks, col_chunks, row_xors, col_xors, new=(), row_outs=(),
          col_outs=(), dtypes=None):
    n_row, n_col = (sum(c[1] for c in chunks) for chunks in (row_chunks, col_chunks))
    tables = tables if new else []
    width = next(iter(rows.values())).shape[1] if rows else held[0].shape[1]
    plan = dict(
        row_chunks=row_chunks, col_chunks=col_chunks, row_xors=row_xors, col_xors=col_xors, n_tables=len(tables),
        row_places=list(rows), col_places=list(cols), aliased=held is not None, new=new, row_outs=row_outs,
        col_outs=col_outs, step=512,
    )
    smem, anywhere, vmem = (pl.BlockSpec(memory_space=m) for m in (pltpu.SMEM, pl.ANY, pltpu.VMEM))
    args = [own, *tables, *rows.values(), *cols.values()]
    in_specs = [smem] * (1 + len(tables)) + [anywhere] * (len(rows) + len(cols))
    out_shape, aliases = [], {}
    if new:
        out_shape.append(pltpu.VMEM((8, 128), jnp.float32))
        if held is not None:
            aliases = {len(args) + k: 1 + k for k in range(3)}
        out_shape += [
            pltpu.VMEM(shape, jnp.bfloat16) for shape in ((n_row, width), (n_col, width), (n_col, n_row))
        ]
    if held is not None:
        args += [pltpu.with_memory_space_constraint(x, pltpu.VMEM) for x in held]
        in_specs += [vmem] * 3
    outs = (*row_outs, *col_outs)
    lengths = [sum(b - a for a, b in out) for out in outs]
    dtypes = dtypes or [jnp.bfloat16] * len(lengths)
    out_shape += [pltpu.VMEM((n, width), dtype) for n, dtype in zip(lengths, dtypes)]
    row_total, col_total = sum(lengths[: len(row_outs)]), sum(lengths[len(row_outs) :])
    area = sum((r1 - r0) * (c1 - c0) for r0, r1, c0, c1 in new)
    flops = 2 * width * (area + row_total * n_col + col_total * n_row)
    outs = list(
        pl.pallas_call(
            functools.partial(tile_kernel, plan),
            in_specs=in_specs,
            out_specs=[vmem] * len(out_shape),
            out_shape=out_shape,
            input_output_aliases=aliases,
            scratch_shapes=[
                pltpu.VMEM(
                    (max(16, sum(c1 - c0 for _, _, c0, c1 in new)), max([128] + [r1 - r0 for r0, r1, _, _ in new])),
                    jnp.bfloat16,
                ),
                pltpu.SemaphoreType.DMA((max(1, len(rows) + len(cols) + len(new)),)),
            ],
            cost_estimate=pl.CostEstimate(flops=flops, bytes_accessed=4 * width * width, transcendentals=2 * area),
            compiler_params=pltpu.CompilerParams(vmem_limit_bytes=20 << 20),
        )(*args)
    )
    loss = outs.pop(0) if new else None
    if new:
        held, outs = outs[:3], outs[3:]
    return loss, held, outs[: len(row_outs)], outs[len(row_outs) :]


def counts(pos_offset, neg_blocks, size):
    blocks = jnp.arange(size, dtype=jnp.int32)
    target = lax.axis_index(AXIS).astype(jnp.int32) + pos_offset.reshape(-1)
    pos = jnp.sum((target[:, None] == blocks).astype(jnp.float32), axis=0)
    neg = jnp.sum((neg_blocks.reshape(-1)[:, None] == blocks).astype(jnp.float32), axis=0)
    return jnp.concatenate([pos, neg])


def add_kernel(starts, *refs):
    *parts, out = refs
    out[...] = sum(
        part[start : start + out.shape[0], :].astype(jnp.float32) for start, part in zip(starts, parts)
    ).astype(out.dtype)


def add(rows, *parts):
    vmem = pl.BlockSpec(memory_space=pltpu.VMEM)
    width = parts[0][0].shape[1]
    return pl.pallas_call(
        functools.partial(add_kernel, [start for _, start in parts]),
        in_specs=[vmem] * len(parts),
        out_specs=vmem,
        out_shape=pltpu.VMEM((rows, width), jnp.bfloat16),
        cost_estimate=pl.CostEstimate(
            flops=rows * width * len(parts), bytes_accessed=4 * rows * width, transcendentals=0
        ),
        compiler_params=pltpu.CompilerParams(vmem_limit_bytes=4 << 20),
    )(*[pltpu.with_memory_space_constraint(part, pltpu.VMEM) for part, _ in parts])


def finish_kernel(n_loss, firsts, in_place, count, start, *refs):
    n_part = len(firsts)
    losses, parts, refs = refs[:n_loss], refs[n_loss : n_loss + n_part], refs[n_loss + n_part + in_place :]
    *outs, total, sem = refs
    rows, n, stores = total.shape[0], 32, []
    for r in range(0, rows, n):
        here = pl.ds(r, n)
        total[here, :] = sum(part[f + r : f + r + n, :].astype(jnp.float32) for f, part in zip(firsts, parts))
        there = outs[-1].at[pl.ds(start + r, n), 0, :]
        stores.append(pltpu.make_async_copy(total.at[here], there, sem.at[len(stores)]))
        stores[-1].start()
    if n_loss:
        outs[-2][0] = jnp.sum(sum(loss[...] for loss in losses)) * (1.0 / count)
    for copy in stores:
        copy.wait()


def finish_rows(rows, parts, length, start=0, into=None, losses=(), count=1):
    width = parts[0][0].shape[1]
    smem, anywhere, vmem = (pl.BlockSpec(memory_space=m) for m in (pltpu.SMEM, pl.ANY, pltpu.VMEM))
    held = [pltpu.with_memory_space_constraint(x, pltpu.VMEM) for x in (*losses, *(block for block, _ in parts))]
    out_shape = [jax.ShapeDtypeStruct((length, 1, width), jnp.float32)]
    out_specs = [anywhere]
    if losses:
        out_shape, out_specs = [jax.ShapeDtypeStruct((1,), jnp.float32), *out_shape], [smem, anywhere]
    in_place = into is not None
    return pl.pallas_call(
        functools.partial(finish_kernel, len(losses), [first for _, first in parts], in_place, count, start),
        in_specs=[vmem] * len(held) + [anywhere] * in_place,
        out_specs=out_specs,
        out_shape=out_shape,
        input_output_aliases={len(held): len(out_shape) - 1} if in_place else {},
        scratch_shapes=[pltpu.VMEM((rows, width), jnp.float32), pltpu.SemaphoreType.DMA((rows // 32,))],
        cost_estimate=pl.CostEstimate(flops=4 * rows * width, bytes_accessed=14 * rows * width, transcendentals=0),
        compiler_params=pltpu.CompilerParams(vmem_limit_bytes=8 << 20),
    )(*held, *([into] if in_place else []))


def step(states, goals, pos_offset, neg_blocks):
    size = lax.axis_size(AXIS)
    length, width = states.shape[0], states.shape[2]
    half = length // 2
    high = size // 2
    inner = []
    bit = size // 4
    while bit > 1:
        inner.append(bit)
        bit //= 2
    across = high ^ (high >> 1)
    blocks = subsets(inner)
    n_block = len(blocks)
    row_xors, col_xors = [0, across], [x ^ side for x in blocks for side in (0, 1)]
    n_row, n_col = len(row_xors) * length, len(col_xors) * length
    last = n_col - 2 * length
    state, goal = states.reshape(length, width), goals.reshape(length, width)
    own = lax.axis_index(AXIS).astype(jnp.int32).reshape(1)

    def outer(i):
        return (i & across) in (0, across)

    mine = [goal]
    for bit in inner:
        mine = mine + [swap(block, bit, size) for block in mine]
    side = [swap(block, 1, size) for block in mine]
    cols = {2 * k * length + p: b for k in range(n_block) for p, b in ((0, mine[k]), (length, side[k]))}
    pair_in = swap(state, across, size, lambda i: not outer(i))
    pair = pair_in + swap(state, across, size, outer)
    table = counts(pos_offset, neg_blocks, size)
    tables = [table, swap(table, across, size)]

    fixed = dict(
        row_xors=row_xors, col_xors=col_xors,
        row_chunks=tuple((k * length, length, k, 0) for k in range(len(row_xors))),
        col_chunks=tuple((k * length, length, k, 0) for k in range(len(col_xors))),
    )

    def arrived(start, end):
        return {p: c for p, c in cols.items() if start <= p < end}

    loss_a, held, _, _ = phase(
        own, tables[:1], {0: state}, arrived(0, 2 * length), None, new=[(0, length, 0, 2 * length)], **fixed
    )
    loss_b, held, _, _ = phase(
        own, tables[:1], {}, arrived(2 * length, last), held, new=[(0, length, 2 * length, last)], **fixed
    )
    loss_c, held, _, _ = phase(own, tables, {length: pair}, {}, held, new=[(length, n_row, 0, last)], **fixed)
    sides, own_sums = {}, {}

    def goal_phase(which, tables, cols, held, new, rows=()):
        pieces = [[(p * length, (p + 1) * length)] for k in which for p in (2 * k + 1, 2 * k)]
        loss, held, row_outs, outs = phase(
            own, tables, {}, cols, held, new=new, row_outs=rows, col_outs=pieces,
            dtypes=[jnp.float32] * len(rows) + [jnp.bfloat16, jnp.float32] * len(which), **fixed,
        )
        sides.update(zip(which, outs[0::2]))
        own_sums.update(zip(which, outs[1::2]))
        return loss, held, row_outs

    top = n_block // 2
    loss_d, held, _ = goal_phase(
        list(range(n_block - 1, top, -1)), tables, arrived(last, n_col), held, [(0, n_row, last, n_col)]
    )
    loss = loss_a + loss_b + loss_c + loss_d
    _, _, (pair_part,), _ = phase(own, [], {}, {}, held, row_outs=[[(length, n_row)]], **fixed)

    back_pair = swap(pair_part, across, size)
    goal_phase([top], [], {}, held, ())
    _, _, (own_part,) = goal_phase(list(range(top)), [], {}, held, (), rows=[[(0, length)]])
    cross = {k: swap(part, 1, size) for k, part in sides.items()}
    loss = loss + swap(loss, 1, size)
    for s in reversed(range(len(inner))):
        loss = loss + swap(loss, inner[s], size)
    losses = [loss, swap(loss, across, size)]
    addends = {k: [(own_sums[k], 0), (cross[k], 0)] for k in range(n_block)}
    halves = {(k, o): [] for k in range(n_block) for o in (0, half)}
    for s in reversed(range(len(inner))):
        for k in reversed(range(1 << s, 2 << s)):
            to = k - (1 << s)
            for o in (0, half):
                piece = add(half, *[(b, o) for b, _ in addends[k]], *[(b, 0) for b in halves[k, o]])
                halves[to, o].append(swap(piece, inner[s], size))
    pieces = [[(block, o) for block, _ in addends[0]] + [(block, 0) for block in halves[0, o]] for o in (0, half)]
    (grad_goals,) = finish_rows(half, pieces[0], length)
    loss_mean, grad_states = finish_rows(
        length, [(own_part, 0), (back_pair, 0)], length, losses=losses, count=size * length
    )
    (grad_goals,) = finish_rows(half, pieces[1], length, start=half, into=grad_goals)
    return (loss_mean, grad_states, grad_goals)


def solution(mesh):
    spec = P("tm", "groups", None)
    return jax.shard_map(
        step,
        mesh=mesh,
        in_specs=(spec,) * 4,
        out_specs=(P("groups"), spec, spec),
        check_vma=False,
    )
```
